256 devices in a mesh: space: 64 (over z, y, core), event: 4 (over x).
Axes of the slice: x: 4, y: 4, z: 8, core: 2. Of those that a mesh axis runs over, the one named last changes fastest.
Arguments:
- rain: bfloat16 [4, 2, 256, 4, 128], P('event', None, 'space'), may hold values from 0.049804688 to 5
- hidden_init: bfloat16 [4, 256, 128, 128], P('event', 'space'), may hold values from -3 to 3
- cell_init: float32 [4, 256, 128, 128], P('event', 'space'), may hold values from -6 to 6
- land_mask: int32 [256, 128], P('space'), may hold values 0 or 1
- hidden_weight: bfloat16 [9, 128, 512], replicated, may hold values from -0.1875 to 0.1875
- rain_weight: bfloat16 [9, 4, 512], replicated, may hold values from -1 to 1
- gate_bias: float32 [512], replicated, may hold values from -3 to 3
- cotangent: float32 [4, 2, 256, 128, 128], P('event', None, 'space'), may hold values from -6 to 6
Outputs:
- final_hidden: bfloat16 [4, 256, 128, 128], P('event', 'space')
- hidden_grad: float32 [4, 256, 128, 128], P('event', 'space')
- hidden_weight_grad: float32 [9, 128, 512], replicated
- rain_weight_grad: float32 [9, 4, 512], replicated
- bias_grad: float32 [512], replicated
The draws below stay inside these ranges and needn't reach their ends.
All inputs are finite; a program needn't handle non-finite values. No bound on the sum of `land_mask` on one device may be relied on, other than what follows from the above.
Results may differ from the reference program's by a relative error of at most 0.0034.
Values may be sent and summed in bfloat16 or wider, within the bound.
No kernel may reach another device: no remote copies, remote signals or barrier semaphores. Data moves between devices by JAX's collectives and lax.ppermute only.
A program may use at most 64 MiB of HBM per device.

```python
import math
import jax
import jax.numpy as jnp
from jax import lax

HC = 128
CIN = 4
COLS = 128
STEPS = 2
ROWS = 256
EVENTS = 4
GATES = 512


def with_ends(entries, key, least, largest):
    extent = entries.shape
    spot = [jax.random.randint(jax.random.fold_in(key, axis), (), 0, extent[axis]) for axis in range(len(extent))]
    entries = entries.at[tuple(spot)].set(least)
    longest = extent.index(max(extent))
    spot[longest] = (spot[longest] + 1) % extent[longest]
    return entries.at[tuple(spot)].set(largest)


def level_of(stream_key, shape, pieces, low, largest):
    def one(axis_at, parts):
        heights = jax.random.uniform(jax.random.fold_in(jax.random.fold_in(stream_key, 6), axis_at), (parts,), jnp.float32, low / len(pieces), largest / len(pieces))
        return jnp.repeat(jnp.exp(heights), shape[axis_at] // parts).reshape((-1,) + (1,) * (len(shape) - axis_at - 1))

    factor_of = one(*pieces[0])
    for cut in pieces[1:]:
        factor_of = factor_of * one(*cut)
    return factor_of


def centred(rng, extent, width, reach, cuts=(), kind=jnp.bfloat16):
    values = width * jax.random.normal(rng, extent, jnp.float32)
    if cuts:
        values = values * level_of(rng, extent, cuts, -0.22, 0.18)
    return jnp.clip(values, -reach, reach).astype(kind)


def setup_inputs(seed: int = 0) -> dict:
    keys = jax.random.split(jax.random.key(seed), 9)
    rain = jnp.clip(jnp.exp(math.log(5.0) - 4.609084 * jax.random.uniform(keys[0], (EVENTS, STEPS, ROWS, CIN, COLS), jnp.float32) ** level_of(keys[0], (EVENTS, STEPS, ROWS, CIN, COLS), ((0, 4), (2, 64)), -0.2, 0.2)), 0.049804688, 5.0).astype(jnp.bfloat16)
    hidden_init = centred(keys[1], (EVENTS, ROWS, COLS, HC), 0.5, 3.0, ((0, 4), (1, 64)))
    cell_init = centred(keys[2], (EVENTS, ROWS, COLS, HC), 1.0, 6.0, ((0, 4), (1, 64)), jnp.float32)
    land_mask = with_ends((jax.random.randint(keys[3], (ROWS, COLS), 0, 4) < 3).astype(jnp.int32), jax.random.fold_in(keys[3], 1), 0, 1)
    hidden_weight = centred(keys[4], (9, HC, GATES), (9 * HC) ** -0.5, 0.1875)
    rain_weight = centred(keys[5], (9, CIN, GATES), (9 * CIN) ** -0.5, 1.0)
    gate_bias = centred(keys[6], (GATES,), 0.5, 3.0, (), jnp.float32)
    cotangent = centred(keys[7], (EVENTS, STEPS, ROWS, COLS, HC), 1.0, 6.0, ((0, 4), (2, 64)), jnp.float32)
    return {"rain": rain, "hidden_init": hidden_init, "cell_init": cell_init, "land_mask": land_mask, "hidden_weight": hidden_weight, "rain_weight": rain_weight, "gate_bias": gate_bias, "cotangent": cotangent}


def forward_gates(hidden_pad, rain_pad, hidden_weight, rain_weight, gate_bias, height, breadth):
    channels = hidden_pad.shape[-1]
    inputs = rain_pad.shape[-1]
    count = hidden_pad.shape[0] * height * breadth
    totals = jnp.zeros((count, hidden_weight.shape[-1]), jnp.float32) + gate_bias[None, :]
    for row_off in range(3):
        for col_off in range(3):
            tap = 3 * row_off + col_off
            hidden_taps = hidden_pad[:, row_off:row_off + height, col_off:col_off + breadth, :].reshape(-1, channels)
            rain_taps = rain_pad[:, row_off:row_off + height, col_off:col_off + breadth, :].reshape(-1, inputs)
            totals = totals + jnp.dot(hidden_taps, hidden_weight[tap], preferred_element_type=jnp.float32)
            totals = totals + jnp.dot(rain_taps, rain_weight[tap], preferred_element_type=jnp.float32)
    return totals


def lstm_update(totals, cell_prev, mask_cells):
    channels = cell_prev.shape[-1]
    input_gate = jax.nn.sigmoid(totals[:, :channels])
    forget_gate = jax.nn.sigmoid(totals[:, channels:2 * channels])
    output_gate = jax.nn.sigmoid(totals[:, 2 * channels:3 * channels])
    candidate = jnp.tanh(totals[:, 3 * channels:])
    cell_new = forget_gate * cell_prev + input_gate * candidate
    hidden_new = mask_cells * output_gate * jnp.tanh(cell_new)
    return (input_gate, forget_gate, output_gate, candidate), cell_new, hidden_new


def gate_grads(gates, cell_prev, cell_new, mask_cells, grad_hidden, grad_cell):
    input_gate, forget_gate, output_gate, candidate = gates
    squash = jnp.tanh(cell_new)
    masked = grad_hidden * mask_cells
    grad_output = masked * squash
    grad_cell = grad_cell + masked * output_gate * (1.0 - squash * squash)
    gate_grad = jnp.concatenate([
        grad_cell * candidate * input_gate * (1.0 - input_gate),
        grad_cell * cell_prev * forget_gate * (1.0 - forget_gate),
        grad_output * output_gate * (1.0 - output_gate),
        grad_cell * input_gate * (1.0 - candidate * candidate)], axis=1).astype(jnp.bfloat16)
    return gate_grad, grad_cell * forget_gate


def weight_terms(hidden_pad, rain_pad, gate_grad, height, breadth):
    dims = (((0,), (0,)), ((), ()))
    channels = hidden_pad.shape[-1]
    inputs = rain_pad.shape[-1]
    hidden_terms = []
    rain_terms = []
    for row_off in range(3):
        for col_off in range(3):
            hidden_taps = hidden_pad[:, row_off:row_off + height, col_off:col_off + breadth, :].reshape(-1, channels)
            rain_taps = rain_pad[:, row_off:row_off + height, col_off:col_off + breadth, :].reshape(-1, inputs)
            hidden_terms.append(lax.dot_general(hidden_taps, gate_grad, dims, preferred_element_type=jnp.float32))
            rain_terms.append(lax.dot_general(rain_taps, gate_grad, dims, preferred_element_type=jnp.float32))
    return jnp.stack(hidden_terms), jnp.stack(rain_terms)


def spread_back(grad_pad, hidden_weight, height, breadth):
    dims = (((1,), (1,)), ((), ()))
    gates_width = grad_pad.shape[-1]
    count = grad_pad.shape[0] * height * breadth
    total = jnp.zeros((count, hidden_weight.shape[1]), jnp.float32)
    for row_off in range(3):
        for col_off in range(3):
            tap = 3 * row_off + col_off
            piece = grad_pad[:, 2 - row_off:2 - row_off + height, 2 - col_off:2 - col_off + breadth, :].reshape(-1, gates_width)
            total = total + lax.dot_general(piece, hidden_weight[tap], dims, preferred_element_type=jnp.float32)
    return total


def reference(rain, hidden_init, cell_init, land_mask, hidden_weight, rain_weight, gate_bias, cotangent):
    mask_cells = land_mask.astype(jnp.float32).reshape(-1, 1)
    finals = []
    grads = []
    grad_w_hidden = jnp.zeros((9, HC, 4 * HC), jnp.float32)
    grad_w_rain = jnp.zeros((9, CIN, 4 * HC), jnp.float32)
    grad_bias = jnp.zeros((4 * HC,), jnp.float32)
    pad_spec = ((0, 0), (1, 1), (1, 1), (0, 0))
    for event in range(EVENTS):
        hidden = hidden_init[event:event + 1]
        cell = cell_init[event:event + 1].reshape(-1, HC)
        stored = []
        for step in range(STEPS):
            hidden_pad = jnp.pad(hidden, pad_spec)
            rain_pad = jnp.pad(jnp.transpose(rain[event:event + 1, step], (0, 1, 3, 2)), pad_spec)
            totals = forward_gates(hidden_pad, rain_pad, hidden_weight, rain_weight, gate_bias, ROWS, COLS)
            gates, cell_new, hidden_new = lstm_update(totals, cell, mask_cells)
            stored.append((hidden_pad, rain_pad, gates, cell, cell_new))
            cell = cell_new
            hidden = hidden_new.astype(jnp.bfloat16).reshape(1, ROWS, COLS, HC)
        finals.append(hidden)
        grad_hidden = cotangent[event:event + 1, STEPS - 1].reshape(-1, HC)
        grad_cell = jnp.zeros((ROWS * COLS, HC), jnp.float32)
        for step in reversed(range(STEPS)):
            hidden_pad, rain_pad, gates, cell_prev, cell_new = stored[step]
            gate_grad, grad_cell = gate_grads(gates, cell_prev, cell_new, mask_cells, grad_hidden, grad_cell)
            hidden_terms, rain_terms = weight_terms(hidden_pad, rain_pad, gate_grad, ROWS, COLS)
            grad_w_hidden = grad_w_hidden + hidden_terms
            grad_w_rain = grad_w_rain + rain_terms
            grad_bias = grad_bias + jnp.sum(gate_grad.astype(jnp.float32), axis=0)
            grad_pad = jnp.pad(gate_grad.reshape(1, ROWS, COLS, 4 * HC), pad_spec)
            grad_hidden = spread_back(grad_pad, hidden_weight, ROWS, COLS)
            if step > 0:
                grad_hidden = grad_hidden + cotangent[event:event + 1, step - 1].reshape(-1, HC)
        grads.append(grad_hidden.reshape(1, ROWS, COLS, HC))
    return (jnp.concatenate(finals, axis=0), jnp.concatenate(grads, axis=0), grad_w_hidden, grad_w_rain, grad_bias)
```

```python
import functools

import jax
import jax.numpy as jnp
from jax import lax
from jax.experimental import pallas as pl
from jax.experimental.pallas import tpu as pltpu
from jax.sharding import PartitionSpec as P

F32 = jnp.float32
BF16 = jnp.bfloat16
NN = (((1,), (0,)), ((), ()))
NT = (((1,), (1,)), ((), ()))
TN = (((0,), (0,)), ((), ()))
SMEM = pl.BlockSpec(memory_space=pltpu.SMEM)
VMEM = pl.BlockSpec(memory_space=pltpu.VMEM)
LINES = 1216


def dot(a, b, dims):
    return lax.dot_general(a, b, dims, preferred_element_type=F32)


def call(body, n_in, outs, scratch=(), aliases=None):
    return pl.pallas_call(
        body,
        in_specs=[SMEM] + [VMEM] * n_in,
        out_specs=[VMEM] * len(outs),
        out_shape=[jax.ShapeDtypeStruct(shape, dtype) for shape, dtype in outs],
        scratch_shapes=[pltpu.VMEM(shape, dtype) for shape, dtype in scratch],
        input_output_aliases=aliases or {},
    )


def sigmoid(x):
    return 0.5 * jnp.tanh(0.5 * x) + 0.5


def fill_columns(rows_ref, wide_ref):
    at = lax.broadcasted_iota(jnp.int32, (128, 128), 0)
    for row in range(6):
        cells = rows_ref[row].astype(F32)
        spot = slice(row * 128, row * 128 + 128)
        before = jnp.where(at == 0, 0.0, pltpu.roll(cells, 1, 0))
        after = jnp.where(at == 127, 0.0, pltpu.roll(cells, 127, 0))
        wide_ref[spot, 0:128] = before.astype(BF16)
        wide_ref[spot, 128:256] = rows_ref[row]
        wide_ref[spot, 256:384] = after.astype(BF16)


def fold_columns(wide):
    at = lax.broadcasted_iota(jnp.int32, (128, 128), 0)
    before = jnp.where(at == 127, 0.0, pltpu.roll(wide[:, 0:128], 127, 0))
    after = jnp.where(at == 0, 0.0, pltpu.roll(wide[:, 256:384], 1, 0))
    return before + wide[:, 128:256] + after


def fill_rain(rows_ref, taps_ref):
    at = lax.broadcasted_iota(jnp.int32, (24, 128), 1)
    rows = rows_ref[...]
    shifted = (
        jnp.where(at == 0, 0.0, pltpu.roll(rows, 1, 1)),
        rows,
        jnp.where(at == 127, 0.0, pltpu.roll(rows, 127, 1)),
    )
    for row in range(4):
        for row_off in range(3):
            for col_off in range(3):
                tap = 3 * row_off + col_off
                first = (row + row_off) * 4
                taps_ref[tap * 4 : tap * 4 + 4, row * 128 : row * 128 + 128] = shifted[col_off][
                    first : first + 4
                ]
    line = lax.broadcasted_iota(jnp.int32, (28, 512), 0)
    taps_ref[36:64, :] = jnp.where(line == 0, 1.0, 0.0)


def add_up_gates(wide_ref, rain_taps, weight_ref, rain_weight_ref, bias_ref, sums_ref):
    sums_ref[...] = dot(wide_ref[0:512, :], weight_ref[0], NN)
    sums_ref[...] += dot(wide_ref[128:640, :], weight_ref[1], NN)
    sums_ref[...] += dot(wide_ref[256:768, :], weight_ref[2], NN)
    sums_ref[...] += dot(rain_taps, rain_weight_ref[...], TN) + bias_ref[...]


def border_kernel(side_ref, hidden_ref, rain_ref, to_a_ref, to_b_ref):
    side = side_ref[0]
    for out_ref, row in ((to_a_ref, 3 * (1 - side)), (to_b_ref, 3 * side)):
        out_ref[0:128, :] = hidden_ref[row]
        rows = jnp.concatenate(
            [rain_ref[0, row].astype(F32), rain_ref[1, row].astype(F32)], axis=0
        )
        out_ref[128:136, :] = rows.astype(BF16)


def first_kernel(
    side_ref, hidden_ref, from_a_ref, from_b_ref, rain_ref, weight_ref, rain_weight_ref, bias_ref,
    cell_ref, land_ref,
    new_ref, to_a_ref, to_b_ref, cell_new_ref, gates_ref, mask_ref, taps0_ref, taps1_ref, wide_ref,
    rows_ref, rain_rows_ref, taps_ref, sums_ref,
):
    side = side_ref[0]
    rows_ref[1:5] = hidden_ref[...]
    rows_ref[5 * (1 - side)] = from_a_ref[0:128, :]
    rows_ref[5 * side] = from_b_ref[0:128, :]
    fill_columns(rows_ref, wide_ref)
    halo_a = from_a_ref[128:136, :].astype(F32)
    halo_b = from_b_ref[128:136, :].astype(F32)
    top = jnp.where(side == 0, halo_b, halo_a)
    bottom = jnp.where(side == 0, halo_a, halo_b)
    for step, out_ref in ((0, taps0_ref), (1, taps1_ref)):
        rain_rows_ref[0:4, :] = top[4 * step : 4 * step + 4]
        for row in range(4):
            rain_rows_ref[4 * row + 4 : 4 * row + 8, :] = rain_ref[step, row].astype(F32)
        rain_rows_ref[20:24, :] = bottom[4 * step : 4 * step + 4]
        fill_rain(rain_rows_ref, taps_ref)
        out_ref[...] = taps_ref[...].astype(BF16)
    land = land_ref[...].astype(F32)
    for row in range(4):
        spread = jnp.broadcast_to(land[row : row + 1, :], (128, 128))
        mask_ref[row * 128 : row * 128 + 128, :] = jnp.transpose(spread)
    add_up_gates(wide_ref, taps0_ref[...], weight_ref, rain_weight_ref, bias_ref, sums_ref)
    for row in range(4):
        spot = slice(row * 128, row * 128 + 128)
        enter = sigmoid(sums_ref[spot, 0:128])
        forget = sigmoid(sums_ref[spot, 128:256])
        leave = sigmoid(sums_ref[spot, 256:384])
        update = jnp.tanh(sums_ref[spot, 384:512])
        gates_ref[spot, 0:128] = enter
        gates_ref[spot, 128:256] = forget
        gates_ref[spot, 256:384] = leave
        gates_ref[spot, 384:512] = update
        cell_new = forget * cell_ref[spot, :] + enter * update
        cell_new_ref[spot, :] = cell_new
        new_ref[row] = (mask_ref[spot, :] * leave * jnp.tanh(cell_new)).astype(BF16)
    to_a_ref[...] = new_ref[3 * (1 - side)]
    to_b_ref[...] = new_ref[3 * side]


def gate_gradients(gates, cell_prev, cell_new, mask, grad_hidden, grad_cell):
    enter, forget, leave, update = gates
    squash = jnp.tanh(cell_new)
    masked = grad_hidden * mask
    grad_cell = grad_cell + masked * leave * (1.0 - squash * squash)
    return (
        (
            grad_cell * update * enter * (1.0 - enter),
            grad_cell * cell_prev * forget * (1.0 - forget),
            masked * squash * leave * (1.0 - leave),
            grad_cell * enter * (1.0 - update * update),
        ),
        grad_cell * forget,
    )


def send_borders(side, grad_ref, weight_ref, edges_ref, to_a_ref, to_b_ref):
    edges_ref[0] = fold_columns(dot(grad_ref[0:128, :], weight_ref[0], NT))
    edges_ref[1] = fold_columns(dot(grad_ref[384:512, :], weight_ref[2], NT))
    to_a_ref[...] = edges_ref[1 - side]
    to_b_ref[...] = edges_ref[side]


def second_kernel(
    side_ref, hidden_ref, from_a_ref, from_b_ref, taps_ref, weight_ref, rain_weight_ref, bias_ref,
    cell_ref, mask_ref, cotangent_ref,
    new_ref, grad_ref, grad_cell_ref, to_a_ref, to_b_ref, wide_ref,
    rows_ref, sums_ref, edges_ref,
):
    side = side_ref[0]
    rows_ref[1:5] = hidden_ref[...]
    rows_ref[5 * (1 - side)] = from_a_ref[...]
    rows_ref[5 * side] = from_b_ref[...]
    fill_columns(rows_ref, wide_ref)
    add_up_gates(wide_ref, taps_ref[...], weight_ref, rain_weight_ref, bias_ref, sums_ref)
    for row in range(4):
        spot = slice(row * 128, row * 128 + 128)
        enter = sigmoid(sums_ref[spot, 0:128])
        forget = sigmoid(sums_ref[spot, 128:256])
        leave = sigmoid(sums_ref[spot, 256:384])
        update = jnp.tanh(sums_ref[spot, 384:512])
        mask = mask_ref[spot, :]
        cell = cell_ref[spot, :]
        cell_new = forget * cell + enter * update
        new_ref[row] = (mask * leave * jnp.tanh(cell_new)).astype(BF16)
        parts, grad_cell = gate_gradients(
            (enter, forget, leave, update), cell, cell_new, mask, cotangent_ref[row], 0.0
        )
        grad_cell_ref[spot, :] = grad_cell
        for part in range(4):
            grad_ref[spot, part * 128 : part * 128 + 128] = parts[part].astype(BF16)
    send_borders(side, grad_ref, weight_ref, edges_ref, to_a_ref, to_b_ref)


def spread_rows(grad_ref, weight_ref, wide_sum_ref):
    wide_sum_ref[...] = dot(grad_ref[...], weight_ref[1], NT)
    wide_sum_ref[0:384, :] += dot(grad_ref[128:512, :], weight_ref[0], NT)
    wide_sum_ref[128:512, :] += dot(grad_ref[0:384, :], weight_ref[2], NT)


def weight_gradients(side, wide_ref, taps_ref, grad_ref, outs, carried):
    for out, (out_ref, old_ref) in enumerate(zip(outs, carried)):
        start = pl.multiple_of((side if out == 0 else 1 - side) * 256, 256)
        grad = grad_ref[:, pl.ds(start, 256)]
        for row_off in range(3):
            total = dot(wide_ref[row_off * 128 : row_off * 128 + 512, :], grad, TN)
            spot = slice(row_off * 384, row_off * 384 + 384)
            for part in range(2):
                piece = total[:, part * 128 : part * 128 + 128]
                if old_ref is not None:
                    piece = piece + old_ref[part, spot, :]
                out_ref[part, spot, :] = piece
        total = dot(taps_ref[...], grad, NN)
        for part in range(2):
            piece = total[:, part * 128 : part * 128 + 128]
            if old_ref is not None:
                piece = piece + old_ref[part, 1152:1216, :]
            out_ref[part, 1152:1216, :] = piece


def third_kernel(
    side_ref, grad_ref, weight_ref, wide_ref, taps_ref,
    kept_ref, given_ref, own_ref,
    wide_sum_ref,
):
    spread_rows(grad_ref, weight_ref, wide_sum_ref)
    for row in range(4):
        own_ref[row] = fold_columns(wide_sum_ref[row * 128 : row * 128 + 128, :])
    weight_gradients(
        side_ref[0], wide_ref, taps_ref, grad_ref, (kept_ref, given_ref), (None, None)
    )


def fourth_kernel(
    side_ref, old_kept_ref, old_given_ref, own_ref, from_a_ref, from_b_ref, cotangent_ref,
    gates_ref, cell_ref, cell_new_ref, mask_ref, grad_cell_ref, weight_ref, wide_ref, taps_ref,
    kept_ref, given_ref, grad_ref, to_a_ref, to_b_ref,
    total_ref, edges_ref,
):
    side = side_ref[0]
    total_ref[...] = own_ref[...] + cotangent_ref[...]
    total_ref[3 * (1 - side)] += from_a_ref[...]
    total_ref[3 * side] += from_b_ref[...]
    for row in range(4):
        spot = slice(row * 128, row * 128 + 128)
        gates = [gates_ref[spot, part * 128 : part * 128 + 128] for part in range(4)]
        parts, _ = gate_gradients(
            gates, cell_ref[spot, :], cell_new_ref[spot, :], mask_ref[spot, :], total_ref[row],
            grad_cell_ref[spot, :],
        )
        for part in range(4):
            grad_ref[spot, part * 128 : part * 128 + 128] = parts[part].astype(BF16)
    weight_gradients(
        side, wide_ref, taps_ref, grad_ref, (kept_ref, given_ref), (old_kept_ref, old_given_ref)
    )
    send_borders(side, grad_ref, weight_ref, edges_ref, to_a_ref, to_b_ref)


def last_kernel(
    side_ref, grad_ref, weight_ref, from_a_ref, from_b_ref, out_ref, wide_sum_ref
):
    side = side_ref[0]
    spread_rows(grad_ref, weight_ref, wide_sum_ref)
    for row in range(4):
        out_ref[row] = fold_columns(wide_sum_ref[row * 128 : row * 128 + 128, :])
    out_ref[3 * (1 - side)] += from_a_ref[...]
    out_ref[3 * side] += from_b_ref[...]


def pair_kernel(side_ref, kept_ref, got_ref, out_ref):
    for part in range(2):
        for piece in range(8):
            spot = slice(piece * 152, piece * 152 + 152)
            out_ref[part * 8 + piece] = (kept_ref[part, spot, :] + got_ref[part, spot, :]).astype(
                BF16
            )


def fold_kernel(side_ref, parts_ref, out_ref):
    total = parts_ref[0].astype(F32)
    for part in range(1, parts_ref.shape[0]):
        total = total + parts_ref[part].astype(F32)
    total = total.astype(BF16)
    for part in range(out_ref.shape[0]):
        out_ref[part] = total


def unpack_kernel(side_ref, mine_ref, other_ref, hidden_ref, rain_ref, bias_ref):
    for half, source_ref in ((side_ref[0], mine_ref), (1 - side_ref[0], other_ref)):
        for part in range(2):
            lanes = pl.ds(pl.multiple_of(half * 256 + part * 128, 128), 128)
            hidden_ref[:, lanes] = source_ref[part, 0:1152, :].astype(F32)
            tail = source_ref[part, 1152:1216, :].astype(F32)
            rain_ref[:, lanes] = tail[0:36]
            bias_ref[:, lanes] = tail[36:37]


def device_groups(deep, wide, across):
    planes = [
        [((z * wide + y) * 2 + core) * across + x for y in range(wide) for x in range(across)]
        for z in range(deep)
        for core in range(2)
    ]
    columns = [[z * wide * 2 + low for z in range(deep)] for low in range(wide * 2)]
    return (planes, columns)


def sum_everywhere(side, kept, given, swap):
    planes, columns = device_groups(8, 4, 4)
    fold = lambda parts, copies: call(fold_kernel, 1, [((copies, 152, 128), BF16)])(side, parts)[0]
    parts = call(pair_kernel, 2, [((16, 152, 128), BF16)])(side, kept, swap(given))[0]
    parts = lax.all_to_all(parts, ("space", "event"), 0, 0, axis_index_groups=planes)
    parts = lax.all_to_all(fold(parts, 8), "space", 0, 0, axis_index_groups=columns)
    parts = lax.all_to_all(fold(parts, 16), ("space", "event"), 0, 0, axis_index_groups=planes)
    mine = parts.reshape(2, LINES, 128)
    return call(
        unpack_kernel, 2, [((1152, 512), F32), ((36, 512), F32), ((1, 512), F32)]
    )(side, mine, swap(mine))


def on_device(
    rain, hidden_init, cell_init, land_mask, hidden_weight, rain_weight, gate_bias, cotangent
):
    size = lax.axis_size("space")
    side = lax.rem(lax.axis_index("space"), 2).astype(jnp.int32)[None]
    near = [(i, i ^ 1) for i in range(size)]
    far = [(i, i + 1) for i in range(1, size - 1, 2)] + [(i + 1, i) for i in range(1, size - 1, 2)]
    swap = lambda x: lax.ppermute(x, "space", near)
    across = lambda x: lax.ppermute(x, "space", far)
    weight = hidden_weight.reshape(3, 384, 512)
    rain_lines = jnp.pad(rain_weight.reshape(36, 512), ((0, 28), (0, 0)))
    bias = gate_bias.reshape(1, 512)
    hidden = hidden_init[0]
    rain = rain[0]
    cell = cell_init.reshape(512, 128)
    row = ((128, 128), F32)

    to_a, to_b = call(border_kernel, 2, [((136, 128), BF16)] * 2)(side, hidden, rain)
    new, to_a, to_b, cell_new, gates, mask, taps0, taps1, wide0 = call(
        first_kernel,
        9,
        [
            ((4, 128, 128), BF16), ((128, 128), BF16), ((128, 128), BF16), ((512, 128), F32),
            ((512, 512), F32), ((512, 128), F32), ((64, 512), BF16), ((64, 512), BF16),
            ((768, 384), BF16),
        ],
        [((6, 128, 128), BF16), ((24, 128), F32), ((64, 512), F32), ((512, 512), F32)],
    )(side, hidden, swap(to_a), across(to_b), rain, weight, rain_lines, bias, cell, land_mask)
    final, grad1, grad_cell, to_a, to_b, wide1 = call(
        second_kernel,
        10,
        [
            ((4, 128, 128), BF16), ((512, 512), BF16), ((512, 128), F32), row, row,
            ((768, 384), BF16),
        ],
        [((6, 128, 128), BF16), ((512, 512), F32), ((2, 128, 128), F32)],
    )(
        side, new, swap(to_a), across(to_b), taps1, weight, rain_lines, bias, cell_new, mask,
        cotangent[0, 1],
    )
    from_a, from_b = (swap(to_a), across(to_b))
    pile = ((2, LINES, 128), F32)
    kept, given, own = call(
        third_kernel, 4, [pile, pile, ((4, 128, 128), F32)], [((512, 384), F32)]
    )(side, grad1, weight, wide1, taps1)
    kept, given, grad0, to_a, to_b = call(
        fourth_kernel,
        14,
        [pile, pile, ((512, 512), BF16), row, row],
        [((4, 128, 128), F32), ((2, 128, 128), F32)],
        {1: 0, 2: 1},
    )(
        side, kept, given, own, from_a, from_b, cotangent[0, 0], gates, cell, cell_new, mask,
        grad_cell, weight, wide0, taps0,
    )
    grad_hidden = call(last_kernel, 4, [((4, 128, 128), F32)], [((512, 384), F32)])(
        side, grad0, weight, swap(to_a), across(to_b)
    )[0]
    grad_w_hidden, grad_w_rain, grad_bias = sum_everywhere(side, kept, given, swap)
    return (
        final[None],
        grad_hidden[None],
        grad_w_hidden.reshape(hidden_weight.shape),
        grad_w_rain.reshape(rain_weight.shape),
        grad_bias.reshape(gate_bias.shape),
    )


def solution(mesh):
    in_specs = (
        P("event", None, "space", None, None),
        P("event", "space", None, None),
        P("event", "space", None, None),
        P("space", None),
        P(),
        P(),
        P(),
        P("event", None, "space", None, None),
    )
    out_specs = (P("event", "space", None, None), P("event", "space", None, None), P(), P(), P())
    return jax.shard_map(
        on_device, mesh=mesh, in_specs=in_specs, out_specs=out_specs, check_vma=False
    )
```

```python
import functools

import jax
import jax.numpy as jnp
from jax import lax
from jax.experimental import pallas as pl
from jax.experimental.pallas import tpu as pltpu
from jax.sharding import PartitionSpec as P

F32 = jnp.float32
BF16 = jnp.bfloat16
NN = (((1,), (0,)), ((), ()))
NT = (((1,), (1,)), ((), ()))
TN = (((0,), (0,)), ((), ()))
SMEM = pl.BlockSpec(memory_space=pltpu.SMEM)
VMEM = pl.BlockSpec(memory_space=pltpu.VMEM)
LINES = 1216


def dot(a, b, dims):
    return lax.dot_general(a, b, dims, preferred_element_type=F32)


def call(body, n_in, outs, scratch=(), aliases=None):
    return pl.pallas_call(
        body,
        in_specs=[SMEM] + [VMEM] * n_in,
        out_specs=[VMEM] * len(outs),
        out_shape=[jax.ShapeDtypeStruct(shape, dtype) for shape, dtype in outs],
        scratch_shapes=[pltpu.VMEM(shape, dtype) for shape, dtype in scratch],
        input_output_aliases=aliases or {},
    )


def sigmoid(x):
    return 0.5 * jnp.tanh(0.5 * x) + 0.5


def fill_columns(rows_ref, wide_ref):
    at = lax.broadcasted_iota(jnp.int32, (128, 128), 0)
    for row in range(6):
        cells = rows_ref[row].astype(F32)
        spot = slice(row * 128, row * 128 + 128)
        before = jnp.where(at == 0, 0.0, pltpu.roll(cells, 1, 0))
        after = jnp.where(at == 127, 0.0, pltpu.roll(cells, 127, 0))
        wide_ref[spot, 0:128] = before.astype(BF16)
        wide_ref[spot, 128:256] = rows_ref[row]
        wide_ref[spot, 256:384] = after.astype(BF16)


def fold_columns(wide):
    at = lax.broadcasted_iota(jnp.int32, (128, 128), 0)
    before = jnp.where(at == 127, 0.0, pltpu.roll(wide[:, 0:128], 127, 0))
    after = jnp.where(at == 0, 0.0, pltpu.roll(wide[:, 256:384], 1, 0))
    return before + wide[:, 128:256] + after


def fill_rain(rows_ref, taps_ref):
    at = lax.broadcasted_iota(jnp.int32, (24, 128), 1)
    rows = rows_ref[...]
    shifted = (
        jnp.where(at == 0, 0.0, pltpu.roll(rows, 1, 1)),
        rows,
        jnp.where(at == 127, 0.0, pltpu.roll(rows, 127, 1)),
    )
    for row in range(4):
        for row_off in range(3):
            for col_off in range(3):
                tap = 3 * row_off + col_off
                first = (row + row_off) * 4
                taps_ref[tap * 4 : tap * 4 + 4, row * 128 : row * 128 + 128] = shifted[col_off][
                    first : first + 4
                ]
    line = lax.broadcasted_iota(jnp.int32, (28, 512), 0)
    taps_ref[36:64, :] = jnp.where(line == 0, 1.0, 0.0)


def add_up_gates(wide_ref, rain_taps, weight_ref, rain_weight_ref, bias_ref, sums_ref):
    sums_ref[...] = dot(wide_ref[0:512, :], weight_ref[0], NN)
    sums_ref[...] += dot(wide_ref[128:640, :], weight_ref[1], NN)
    sums_ref[...] += dot(wide_ref[256:768, :], weight_ref[2], NN)
    sums_ref[...] += dot(rain_taps, rain_weight_ref[...], TN) + bias_ref[...]


def border_kernel(side_ref, hidden_ref, rain_ref, to_a_ref, to_b_ref):
    side = side_ref[0]
    for out_ref, row in ((to_a_ref, 3 * (1 - side)), (to_b_ref, 3 * side)):
        out_ref[0:128, :] = hidden_ref[row]
        rows = jnp.concatenate(
            [rain_ref[0, row].astype(F32), rain_ref[1, row].astype(F32)], axis=0
        )
        out_ref[128:136, :] = rows.astype(BF16)


def first_kernel(
    side_ref, hidden_ref, from_a_ref, from_b_ref, rain_ref, weight_ref, rain_weight_ref, bias_ref,
    cell_ref, land_ref,
    new_ref, to_a_ref, to_b_ref, cell_new_ref, gates_ref, mask_ref, taps0_ref, taps1_ref, wide_ref,
    rows_ref, rain_rows_ref, taps_ref, sums_ref,
):
    side = side_ref[0]
    rows_ref[1:5] = hidden_ref[...]
    rows_ref[5 * (1 - side)] = from_a_ref[0:128, :]
    rows_ref[5 * side] = from_b_ref[0:128, :]
    fill_columns(rows_ref, wide_ref)
    halo_a = from_a_ref[128:136, :].astype(F32)
    halo_b = from_b_ref[128:136, :].astype(F32)
    top = jnp.where(side == 0, halo_b, halo_a)
    bottom = jnp.where(side == 0, halo_a, halo_b)
    for step, out_ref in ((0, taps0_ref), (1, taps1_ref)):
        rain_rows_ref[0:4, :] = top[4 * step : 4 * step + 4]
        for row in range(4):
            rain_rows_ref[4 * row + 4 : 4 * row + 8, :] = rain_ref[step, row].astype(F32)
        rain_rows_ref[20:24, :] = bottom[4 * step : 4 * step + 4]
        fill_rain(rain_rows_ref, taps_ref)
        out_ref[...] = taps_ref[...].astype(BF16)
    land = land_ref[...].astype(F32)
    for row in range(4):
        spread = jnp.broadcast_to(land[row : row + 1, :], (128, 128))
        mask_ref[row * 128 : row * 128 + 128, :] = jnp.transpose(spread)
    add_up_gates(wide_ref, taps0_ref[...], weight_ref, rain_weight_ref, bias_ref, sums_ref)
    for row in range(4):
        spot = slice(row * 128, row * 128 + 128)
        enter = sigmoid(sums_ref[spot, 0:128])
        forget = sigmoid(sums_ref[spot, 128:256])
        leave = sigmoid(sums_ref[spot, 256:384])
        update = jnp.tanh(sums_ref[spot, 384:512])
        gates_ref[spot, 0:128] = enter
        gates_ref[spot, 128:256] = forget
        gates_ref[spot, 256:384] = leave
        gates_ref[spot, 384:512] = update
        cell_new = forget * cell_ref[spot, :] + enter * update
        cell_new_ref[spot, :] = cell_new
        new_ref[row] = (mask_ref[spot, :] * leave * jnp.tanh(cell_new)).astype(BF16)
    to_a_ref[...] = new_ref[3 * (1 - side)]
    to_b_ref[...] = new_ref[3 * side]


def gate_gradients(gates, cell_prev, cell_new, mask, grad_hidden, grad_cell):
    enter, forget, leave, update = gates
    squash = jnp.tanh(cell_new)
    masked = grad_hidden * mask
    grad_cell = grad_cell + masked * leave * (1.0 - squash * squash)
    return (
        (
            grad_cell * update * enter * (1.0 - enter),
            grad_cell * cell_prev * forget * (1.0 - forget),
            masked * squash * leave * (1.0 - leave),
            grad_cell * enter * (1.0 - update * update),
        ),
        grad_cell * forget,
    )


def send_borders(side, grad_ref, weight_ref, edges_ref, to_a_ref, to_b_ref):
    edges_ref[0] = fold_columns(dot(grad_ref[0:128, :], weight_ref[0], NT))
    edges_ref[1] = fold_columns(dot(grad_ref[384:512, :], weight_ref[2], NT))
    to_a_ref[...] = edges_ref[1 - side]
    to_b_ref[...] = edges_ref[side]


def second_kernel(
    side_ref, hidden_ref, from_a_ref, from_b_ref, taps_ref, weight_ref, rain_weight_ref, bias_ref,
    cell_ref, mask_ref, cotangent_ref,
    new_ref, grad_ref, grad_cell_ref, to_a_ref, to_b_ref, wide_ref,
    rows_ref, sums_ref, edges_ref,
):
    side = side_ref[0]
    rows_ref[1:5] = hidden_ref[...]
    rows_ref[5 * (1 - side)] = from_a_ref[...]
    rows_ref[5 * side] = from_b_ref[...]
    fill_columns(rows_ref, wide_ref)
    add_up_gates(wide_ref, taps_ref[...], weight_ref, rain_weight_ref, bias_ref, sums_ref)
    for row in range(4):
        spot = slice(row * 128, row * 128 + 128)
        enter = sigmoid(sums_ref[spot, 0:128])
        forget = sigmoid(sums_ref[spot, 128:256])
        leave = sigmoid(sums_ref[spot, 256:384])
        update = jnp.tanh(sums_ref[spot, 384:512])
        mask = mask_ref[spot, :]
        cell = cell_ref[spot, :]
        cell_new = forget * cell + enter * update
        new_ref[row] = (mask * leave * jnp.tanh(cell_new)).astype(BF16)
        parts, grad_cell = gate_gradients(
            (enter, forget, leave, update), cell, cell_new, mask, cotangent_ref[row], 0.0
        )
        grad_cell_ref[spot, :] = grad_cell
        for part in range(4):
            grad_ref[spot, part * 128 : part * 128 + 128] = parts[part].astype(BF16)
    send_borders(side, grad_ref, weight_ref, edges_ref, to_a_ref, to_b_ref)


def spread_rows(grad_ref, weight_ref, wide_sum_ref):
    wide_sum_ref[...] = dot(grad_ref[...], weight_ref[1], NT)
    wide_sum_ref[0:384, :] += dot(grad_ref[128:512, :], weight_ref[0], NT)
    wide_sum_ref[128:512, :] += dot(grad_ref[0:384, :], weight_ref[2], NT)


def weight_gradients(side, wide_ref, taps_ref, grad_ref, outs, carried):
    for out, (out_ref, old_ref) in enumerate(zip(outs, carried)):
        start = pl.multiple_of((side if out == 0 else 1 - side) * 256, 256)
        grad = grad_ref[:, pl.ds(start, 256)]
        for row_off in range(3):
            total = dot(wide_ref[row_off * 128 : row_off * 128 + 512, :], grad, TN)
            spot = slice(row_off * 384, row_off * 384 + 384)
            for part in range(2):
                piece = total[:, part * 128 : part * 128 + 128]
                if old_ref is not None:
                    piece = piece + old_ref[part, spot, :]
                out_ref[part, spot, :] = piece
        total = dot(taps_ref[...], grad, NN)
        for part in range(2):
            piece = total[:, part * 128 : part * 128 + 128]
            if old_ref is not None:
                piece = piece + old_ref[part, 1152:1216, :]
            out_ref[part, 1152:1216, :] = piece


def third_kernel(
    side_ref, grad_ref, weight_ref, wide_ref, taps_ref,
    kept_ref, given_ref, own_ref,
    wide_sum_ref,
):
    spread_rows(grad_ref, weight_ref, wide_sum_ref)
    for row in range(4):
        own_ref[row] = fold_columns(wide_sum_ref[row * 128 : row * 128 + 128, :])
    weight_gradients(
        side_ref[0], wide_ref, taps_ref, grad_ref, (kept_ref, given_ref), (None, None)
    )


def fourth_kernel(
    side_ref, old_kept_ref, old_given_ref, own_ref, from_a_ref, from_b_ref, cotangent_ref,
    gates_ref, cell_ref, cell_new_ref, mask_ref, grad_cell_ref, weight_ref, wide_ref, taps_ref,
    kept_ref, given_ref, grad_ref, to_a_ref, to_b_ref,
    total_ref, edges_ref,
):
    side = side_ref[0]
    total_ref[...] = own_ref[...] + cotangent_ref[...]
    total_ref[3 * (1 - side)] += from_a_ref[...]
    total_ref[3 * side] += from_b_ref[...]
    for row in range(4):
        spot = slice(row * 128, row * 128 + 128)
        gates = [gates_ref[spot, part * 128 : part * 128 + 128] for part in range(4)]
        parts, _ = gate_gradients(
            gates, cell_ref[spot, :], cell_new_ref[spot, :], mask_ref[spot, :], total_ref[row],
            grad_cell_ref[spot, :],
        )
        for part in range(4):
            grad_ref[spot, part * 128 : part * 128 + 128] = parts[part].astype(BF16)
    weight_gradients(
        side, wide_ref, taps_ref, grad_ref, (kept_ref, given_ref), (old_kept_ref, old_given_ref)
    )
    send_borders(side, grad_ref, weight_ref, edges_ref, to_a_ref, to_b_ref)


def last_kernel(
    side_ref, grad_ref, weight_ref, from_a_ref, from_b_ref, out_ref, wide_sum_ref
):
    side = side_ref[0]
    spread_rows(grad_ref, weight_ref, wide_sum_ref)
    for row in range(4):
        out_ref[row] = fold_columns(wide_sum_ref[row * 128 : row * 128 + 128, :])
    out_ref[3 * (1 - side)] += from_a_ref[...]
    out_ref[3 * side] += from_b_ref[...]


def pair_kernel(side_ref, kept_ref, got_ref, out_ref):
    for part in range(2):
        for piece in range(8):
            spot = slice(piece * 152, piece * 152 + 152)
            out_ref[part * 8 + piece] = (kept_ref[part, spot, :] + got_ref[part, spot, :]).astype(
                BF16
            )


def fold_kernel(side_ref, parts_ref, out_ref):
    total = parts_ref[0].astype(F32)
    for part in range(1, parts_ref.shape[0]):
        total = total + parts_ref[part].astype(F32)
    total = total.astype(BF16)
    for part in range(out_ref.shape[0]):
        out_ref[part] = total


def unpack_kernel(side_ref, mine_ref, other_ref, hidden_ref, rain_ref, bias_ref):
    for half, source_ref in ((side_ref[0], mine_ref), (1 - side_ref[0], other_ref)):
        for part in range(2):
            lanes = pl.ds(pl.multiple_of(half * 256 + part * 128, 128), 128)
            hidden_ref[:, lanes] = source_ref[part, 0:1152, :].astype(F32)
            tail = source_ref[part, 1152:1216, :].astype(F32)
            for tap in range(9):
                rain_ref[tap, :, lanes] = tail[tap * 4 : tap * 4 + 4]
            bias_ref[:, lanes] = tail[36:37]


def device_groups(deep, wide, across):
    planes = [
        [((z * wide + y) * 2 + core) * across + x for y in range(wide) for x in range(across)]
        for z in range(deep)
        for core in range(2)
    ]
    columns = [[z * wide * 2 + low for z in range(deep)] for low in range(wide * 2)]
    return (planes, columns)


def sum_everywhere(side, kept, got, swap, beside):
    planes, columns = device_groups(8, 4, 4)
    fold = lambda parts, copies: call(fold_kernel, 1, [((copies, 152, 128), BF16)])(side, parts)[0]
    parts = call(pair_kernel, 2, [((16, 152, 128), BF16)])(side, kept, got)[0]
    parts = lax.all_to_all(parts, ("space", "event"), 0, 0, axis_index_groups=planes)
    parts = lax.all_to_all(fold(parts, 8), "space", 0, 0, axis_index_groups=columns)
    parts = lax.all_to_all(fold(parts, 16), ("space", "event"), 0, 0, axis_index_groups=planes)
    mine = parts.reshape(2, LINES, 128)
    mine, held = lax.optimization_barrier((mine, beside[0]))
    other, hidden = swap(mine), beside[1](held)
    return hidden, *call(
        unpack_kernel, 2, [((1152, 512), F32), ((9, 4, 512), F32), ((1, 512), F32)]
    )(side, mine, other)


def on_device(
    rain, hidden_init, cell_init, land_mask, hidden_weight, rain_weight, gate_bias, cotangent
):
    size = lax.axis_size("space")
    side = lax.rem(lax.axis_index("space"), 2).astype(jnp.int32)[None]
    near = [(i, i ^ 1) for i in range(size)]
    far = [(i, i + 1) for i in range(1, size - 1, 2)] + [(i + 1, i) for i in range(1, size - 1, 2)]
    swap = lambda x: lax.ppermute(x, "space", near)
    across = lambda x: lax.ppermute(x, "space", far)
    weight = hidden_weight.reshape(3, 384, 512)
    rain_lines = jnp.pad(rain_weight.reshape(36, 512), ((0, 28), (0, 0)))
    bias = gate_bias.reshape(1, 512)
    hidden = hidden_init[0]
    rain = rain[0]
    cell = cell_init.reshape(512, 128)
    row = ((128, 128), F32)

    to_a, to_b = call(border_kernel, 2, [((136, 128), BF16)] * 2)(side, hidden, rain)
    new, to_a, to_b, cell_new, gates, mask, taps0, taps1, wide0 = call(
        first_kernel,
        9,
        [
            ((4, 128, 128), BF16), ((128, 128), BF16), ((128, 128), BF16), ((512, 128), F32),
            ((512, 512), F32), ((512, 128), F32), ((64, 512), BF16), ((64, 512), BF16),
            ((768, 384), BF16),
        ],
        [((6, 128, 128), BF16), ((24, 128), F32), ((64, 512), F32), ((512, 512), F32)],
    )(side, hidden, swap(to_a), across(to_b), rain, weight, rain_lines, bias, cell, land_mask)
    final, grad1, grad_cell, to_a, to_b, wide1 = call(
        second_kernel,
        10,
        [
            ((4, 128, 128), BF16), ((512, 512), BF16), ((512, 128), F32), row, row,
            ((768, 384), BF16),
        ],
        [((6, 128, 128), BF16), ((512, 512), F32), ((2, 128, 128), F32)],
    )(
        side, new, swap(to_a), across(to_b), taps1, weight, rain_lines, bias, cell_new, mask,
        cotangent[0, 1],
    )
    from_a, from_b = (swap(to_a), across(to_b))
    pile = ((2, LINES, 128), F32)
    kept, given, own = call(
        third_kernel, 4, [pile, pile, ((4, 128, 128), F32)], [((512, 384), F32)]
    )(side, grad1, weight, wide1, taps1)
    kept, given, grad0, to_a, to_b = call(
        fourth_kernel,
        14,
        [pile, pile, ((512, 512), BF16), row, row],
        [((4, 128, 128), F32), ((2, 128, 128), F32)],
        {1: 0, 2: 1},
    )(
        side, kept, given, own, from_a, from_b, cotangent[0, 0], gates, cell, cell_new, mask,
        grad_cell, weight, wide0, taps0,
    )
    got, from_a, from_b = lax.optimization_barrier((swap(given), swap(to_a), across(to_b)))
    last = lambda grad: call(last_kernel, 4, [((4, 128, 128), F32)], [((512, 384), F32)])(
        side, grad, weight, from_a, from_b
    )[0]
    grad_hidden, grad_w_hidden, grad_w_rain, grad_bias = sum_everywhere(
        side, kept, got, swap, (grad0, last)
    )
    return (
        final[None],
        grad_hidden[None],
        grad_w_hidden.reshape(hidden_weight.shape),
        grad_w_rain,
        grad_bias.reshape(gate_bias.shape),
    )


def solution(mesh):
    in_specs = (
        P("event", None, "space", None, None),
        P("event", "space", None, None),
        P("event", "space", None, None),
        P("space", None),
        P(),
        P(),
        P(),
        P("event", None, "space", None, None),
    )
    out_specs = (P("event", "space", None, None), P("event", "space", None, None), P(), P(), P())
    return jax.shard_map(
        on_device, mesh=mesh, in_specs=in_specs, out_specs=out_specs, check_vma=False
    )
```

```python
import functools

import jax
import jax.numpy as jnp
from jax import lax
from jax.experimental import pallas as pl
from jax.experimental.pallas import tpu as pltpu
from jax.sharding import PartitionSpec as P

F32 = jnp.float32
BF16 = jnp.bfloat16
NN = (((1,), (0,)), ((), ()))
NT = (((1,), (1,)), ((), ()))
TN = (((0,), (0,)), ((), ()))
SMEM = pl.BlockSpec(memory_space=pltpu.SMEM)
VMEM = pl.BlockSpec(memory_space=pltpu.VMEM)
LINES = 1200
PIECE = 24


def dot(a, b, dims):
    return lax.dot_general(a, b, dims, preferred_element_type=F32)


def call(body, n_in, outs, scratch=(), aliases=None):
    return pl.pallas_call(
        body,
        in_specs=[SMEM] + [VMEM] * n_in,
        out_specs=[VMEM] * len(outs),
        out_shape=[jax.ShapeDtypeStruct(shape, dtype) for shape, dtype in outs],
        scratch_shapes=[pltpu.VMEM(shape, dtype) for shape, dtype in scratch],
        input_output_aliases=aliases or {},
    )


def sigmoid(x):
    return 0.5 * jnp.tanh(0.5 * x) + 0.5


def fill_columns(rows_ref, wide_ref):
    at = lax.broadcasted_iota(jnp.int32, (128, 128), 0)
    for row in range(6):
        cells = rows_ref[row].astype(F32)
        spot = slice(row * 128, row * 128 + 128)
        before = jnp.where(at == 0, 0.0, pltpu.roll(cells, 1, 0))
        after = jnp.where(at == 127, 0.0, pltpu.roll(cells, 127, 0))
        wide_ref[spot, 0:128] = before.astype(BF16)
        wide_ref[spot, 128:256] = rows_ref[row]
        wide_ref[spot, 256:384] = after.astype(BF16)


def fold_columns(wide):
    at = lax.broadcasted_iota(jnp.int32, (128, 128), 0)
    before = jnp.where(at == 127, 0.0, pltpu.roll(wide[:, 0:128], 127, 0))
    after = jnp.where(at == 0, 0.0, pltpu.roll(wide[:, 256:384], 1, 0))
    return before + wide[:, 128:256] + after


def fill_rain(rows_ref, taps_ref):
    at = lax.broadcasted_iota(jnp.int32, (24, 128), 1)
    rows = rows_ref[...]
    shifted = (
        jnp.where(at == 0, 0.0, pltpu.roll(rows, 1, 1)),
        rows,
        jnp.where(at == 127, 0.0, pltpu.roll(rows, 127, 1)),
    )
    for row in range(4):
        for row_off in range(3):
            for col_off in range(3):
                tap = 3 * row_off + col_off
                first = (row + row_off) * 4
                taps_ref[tap * 4 : tap * 4 + 4, row * 128 : row * 128 + 128] = shifted[col_off][
                    first : first + 4
                ]
    line = lax.broadcasted_iota(jnp.int32, (28, 512), 0)
    taps_ref[36:64, :] = jnp.where(line == 0, 1.0, 0.0)


def add_up_gates(wide_ref, rain_taps, weight_ref, rain_weight_ref, bias_ref, sums_ref):
    sums_ref[...] = dot(wide_ref[0:512, :], weight_ref[0], NN)
    sums_ref[...] += dot(wide_ref[128:640, :], weight_ref[1], NN)
    sums_ref[...] += dot(wide_ref[256:768, :], weight_ref[2], NN)
    sums_ref[...] += dot(rain_taps, rain_weight_ref[...], TN) + bias_ref[...]


def border_kernel(side_ref, hidden_ref, rain_ref, to_a_ref, to_b_ref):
    side = side_ref[0]
    for out_ref, row in ((to_a_ref, 3 * (1 - side)), (to_b_ref, 3 * side)):
        out_ref[0:128, :] = hidden_ref[row]
        rows = jnp.concatenate(
            [rain_ref[0, row].astype(F32), rain_ref[1, row].astype(F32)], axis=0
        )
        out_ref[128:136, :] = rows.astype(BF16)


def first_kernel(
    side_ref, hidden_ref, from_a_ref, from_b_ref, rain_ref, weight_ref, rain_weight_ref, bias_ref,
    cell_ref, land_ref,
    new_ref, to_a_ref, to_b_ref, cell_new_ref, gates_ref, mask_ref, taps0_ref, taps1_ref, wide_ref,
    rows_ref, rain_rows_ref, taps_ref, sums_ref,
):
    side = side_ref[0]
    rows_ref[1:5] = hidden_ref[...]
    rows_ref[5 * (1 - side)] = from_a_ref[0:128, :]
    rows_ref[5 * side] = from_b_ref[0:128, :]
    fill_columns(rows_ref, wide_ref)
    halo_a = from_a_ref[128:136, :].astype(F32)
    halo_b = from_b_ref[128:136, :].astype(F32)
    top = jnp.where(side == 0, halo_b, halo_a)
    bottom = jnp.where(side == 0, halo_a, halo_b)
    for step, out_ref in ((0, taps0_ref), (1, taps1_ref)):
        rain_rows_ref[0:4, :] = top[4 * step : 4 * step + 4]
        for row in range(4):
            rain_rows_ref[4 * row + 4 : 4 * row + 8, :] = rain_ref[step, row].astype(F32)
        rain_rows_ref[20:24, :] = bottom[4 * step : 4 * step + 4]
        fill_rain(rain_rows_ref, taps_ref)
        out_ref[...] = taps_ref[...].astype(BF16)
    land = land_ref[...].astype(F32)
    for row in range(4):
        spread = jnp.broadcast_to(land[row : row + 1, :], (128, 128))
        mask_ref[row * 128 : row * 128 + 128, :] = jnp.transpose(spread)
    add_up_gates(wide_ref, taps0_ref[...], weight_ref, rain_weight_ref, bias_ref, sums_ref)
    for row in range(4):
        spot = slice(row * 128, row * 128 + 128)
        enter = sigmoid(sums_ref[spot, 0:128])
        forget = sigmoid(sums_ref[spot, 128:256])
        leave = sigmoid(sums_ref[spot, 256:384])
        update = jnp.tanh(sums_ref[spot, 384:512])
        gates_ref[spot, 0:128] = enter
        gates_ref[spot, 128:256] = forget
        gates_ref[spot, 256:384] = leave
        gates_ref[spot, 384:512] = update
        cell_new = forget * cell_ref[spot, :] + enter * update
        cell_new_ref[spot, :] = cell_new
        new_ref[row] = (mask_ref[spot, :] * leave * jnp.tanh(cell_new)).astype(BF16)
    to_a_ref[...] = new_ref[3 * (1 - side)]
    to_b_ref[...] = new_ref[3 * side]


def gate_gradients(gates, cell_prev, cell_new, mask, grad_hidden, grad_cell):
    enter, forget, leave, update = gates
    squash = jnp.tanh(cell_new)
    masked = grad_hidden * mask
    grad_cell = grad_cell + masked * leave * (1.0 - squash * squash)
    return (
        (
            grad_cell * update * enter * (1.0 - enter),
            grad_cell * cell_prev * forget * (1.0 - forget),
            masked * squash * leave * (1.0 - leave),
            grad_cell * enter * (1.0 - update * update),
        ),
        grad_cell * forget,
    )


def send_borders(side, grad_ref, weight_ref, edges_ref, to_a_ref, to_b_ref):
    edges_ref[0] = fold_columns(dot(grad_ref[0:128, :], weight_ref[0], NT))
    edges_ref[1] = fold_columns(dot(grad_ref[384:512, :], weight_ref[2], NT))
    to_a_ref[...] = edges_ref[1 - side]
    to_b_ref[...] = edges_ref[side]


def second_kernel(
    side_ref, hidden_ref, from_a_ref, from_b_ref, taps_ref, weight_ref, rain_weight_ref, bias_ref,
    cell_ref, mask_ref, cotangent_ref,
    new_ref, grad_ref, grad_cell_ref, to_a_ref, to_b_ref, wide_ref,
    rows_ref, sums_ref, edges_ref,
):
    side = side_ref[0]
    rows_ref[1:5] = hidden_ref[...]
    rows_ref[5 * (1 - side)] = from_a_ref[...]
    rows_ref[5 * side] = from_b_ref[...]
    fill_columns(rows_ref, wide_ref)
    add_up_gates(wide_ref, taps_ref[...], weight_ref, rain_weight_ref, bias_ref, sums_ref)
    for row in range(4):
        spot = slice(row * 128, row * 128 + 128)
        enter = sigmoid(sums_ref[spot, 0:128])
        forget = sigmoid(sums_ref[spot, 128:256])
        leave = sigmoid(sums_ref[spot, 256:384])
        update = jnp.tanh(sums_ref[spot, 384:512])
        mask = mask_ref[spot, :]
        cell = cell_ref[spot, :]
        cell_new = forget * cell + enter * update
        new_ref[row] = (mask * leave * jnp.tanh(cell_new)).astype(BF16)
        parts, grad_cell = gate_gradients(
            (enter, forget, leave, update), cell, cell_new, mask, cotangent_ref[row], 0.0
        )
        grad_cell_ref[spot, :] = grad_cell
        for part in range(4):
            grad_ref[spot, part * 128 : part * 128 + 128] = parts[part].astype(BF16)
    send_borders(side, grad_ref, weight_ref, edges_ref, to_a_ref, to_b_ref)


def spread_rows(grad_ref, weight_ref, wide_sum_ref):
    wide_sum_ref[...] = dot(grad_ref[...], weight_ref[1], NT)
    wide_sum_ref[0:384, :] += dot(grad_ref[128:512, :], weight_ref[0], NT)
    wide_sum_ref[128:512, :] += dot(grad_ref[0:384, :], weight_ref[2], NT)


def weight_gradients(side, wide_ref, taps_ref, grad_ref, outs, carried):
    for out, (out_ref, old_ref) in enumerate(zip(outs, carried)):
        start = pl.multiple_of((side if out == 0 else 1 - side) * 256, 256)
        grad = grad_ref[:, pl.ds(start, 256)]
        for row_off in range(3):
            total = dot(wide_ref[row_off * 128 : row_off * 128 + 512, :], grad, TN)
            spot = slice(row_off * 384, row_off * 384 + 384)
            for part in range(2):
                piece = total[:, part * 128 : part * 128 + 128]
                if old_ref is not None:
                    piece = piece + old_ref[part, spot, :]
                out_ref[part, spot, :] = piece
        total = dot(taps_ref[...], grad, NN)
        for part in range(2):
            piece = total[0 : LINES - 1152, part * 128 : part * 128 + 128]
            if old_ref is not None:
                piece = piece + old_ref[part, 1152:LINES, :]
            out_ref[part, 1152:LINES, :] = piece


def third_kernel(
    side_ref, grad_ref, weight_ref, wide_ref, taps_ref,
    kept_ref, given_ref, own_ref,
    wide_sum_ref,
):
    spread_rows(grad_ref, weight_ref, wide_sum_ref)
    for row in range(4):
        own_ref[row] = fold_columns(wide_sum_ref[row * 128 : row * 128 + 128, :])
    weight_gradients(
        side_ref[0], wide_ref, taps_ref, grad_ref, (kept_ref, given_ref), (None, None)
    )


def fourth_kernel(
    side_ref, old_kept_ref, old_given_ref, own_ref, from_a_ref, from_b_ref, cotangent_ref,
    gates_ref, cell_ref, cell_new_ref, mask_ref, grad_cell_ref, weight_ref, wide_ref, taps_ref,
    kept_ref, given_ref, grad_ref, to_a_ref, to_b_ref,
    total_ref, edges_ref,
):
    side = side_ref[0]
    total_ref[...] = own_ref[...] + cotangent_ref[...]
    total_ref[3 * (1 - side)] += from_a_ref[...]
    total_ref[3 * side] += from_b_ref[...]
    for row in range(4):
        spot = slice(row * 128, row * 128 + 128)
        gates = [gates_ref[spot, part * 128 : part * 128 + 128] for part in range(4)]
        parts, _ = gate_gradients(
            gates, cell_ref[spot, :], cell_new_ref[spot, :], mask_ref[spot, :], total_ref[row],
            grad_cell_ref[spot, :],
        )
        for part in range(4):
            grad_ref[spot, part * 128 : part * 128 + 128] = parts[part].astype(BF16)
    weight_gradients(
        side, wide_ref, taps_ref, grad_ref, (kept_ref, given_ref), (old_kept_ref, old_given_ref)
    )
    send_borders(side, grad_ref, weight_ref, edges_ref, to_a_ref, to_b_ref)


def last_kernel(
    side_ref, grad_ref, weight_ref, from_a_ref, from_b_ref, out_ref, wide_sum_ref
):
    side = side_ref[0]
    spread_rows(grad_ref, weight_ref, wide_sum_ref)
    for row in range(4):
        out_ref[row] = fold_columns(wide_sum_ref[row * 128 : row * 128 + 128, :])
    out_ref[3 * (1 - side)] += from_a_ref[...]
    out_ref[3 * side] += from_b_ref[...]


def pair_kernel(side_ref, kept_ref, got_ref, out_ref):
    live = LINES // PIECE
    for part in range(2):
        for piece in range(live):
            spot = slice(piece * PIECE, piece * PIECE + PIECE)
            out_ref[part * live + piece] = (
                kept_ref[part, spot, :] + got_ref[part, spot, :]
            ).astype(BF16)
    for piece in range(2 * live, out_ref.shape[0]):
        out_ref[piece] = jnp.zeros((PIECE, 128), BF16)


def fold_kernel(side_ref, parts_ref, out_ref):
    total = parts_ref[0].astype(F32)
    for part in range(1, parts_ref.shape[0]):
        total = total + parts_ref[part].astype(F32)
    total = total.astype(BF16)
    for part in range(out_ref.shape[0]):
        out_ref[part] = total


def unpack_kernel(side_ref, mine_ref, other_ref, hidden_ref, rain_ref, bias_ref):
    for half, source_ref in ((side_ref[0], mine_ref), (1 - side_ref[0], other_ref)):
        for part in range(2):
            lanes = pl.ds(pl.multiple_of(half * 256 + part * 128, 128), 128)
            first = part * LINES
            hidden_ref[:, lanes] = source_ref[first : first + 1152, :].astype(F32)
            tail = source_ref[first + 1152 : first + LINES, :].astype(F32)
            for tap in range(9):
                rain_ref[tap, :, lanes] = tail[tap * 4 : tap * 4 + 4]
            bias_ref[:, lanes] = tail[36:37]


def device_groups(chips, across):
    return [
        [(chip * 2 + core) * across + x for chip in range(chips) for x in range(across)]
        for core in range(2)
    ]


def sum_everywhere(side, kept, got, swap, beside):
    groups = device_groups(32, 4)
    pieces = [((128, PIECE, 128), BF16)]
    spread = lambda x: lax.all_to_all(x, ("space", "event"), 0, 0, axis_index_groups=groups)
    parts = spread(call(pair_kernel, 2, pieces)(side, kept, got)[0])
    parts = spread(call(fold_kernel, 1, pieces)(side, parts)[0])
    mine = parts.reshape(128 * PIECE, 128)
    mine, held = lax.optimization_barrier((mine, beside[0]))
    other, hidden = swap(mine), beside[1](held)
    return hidden, *call(
        unpack_kernel, 2, [((1152, 512), F32), ((9, 4, 512), F32), ((1, 512), F32)]
    )(side, mine, other)


def on_device(
    rain, hidden_init, cell_init, land_mask, hidden_weight, rain_weight, gate_bias, cotangent
):
    size = lax.axis_size("space")
    side = lax.rem(lax.axis_index("space"), 2).astype(jnp.int32)[None]
    near = [(i, i ^ 1) for i in range(size)]
    far = [(i, i + 1) for i in range(1, size - 1, 2)] + [(i + 1, i) for i in range(1, size - 1, 2)]
    swap = lambda x: lax.ppermute(x, "space", near)
    across = lambda x: lax.ppermute(x, "space", far)
    weight = hidden_weight.reshape(3, 384, 512)
    rain_lines = jnp.pad(rain_weight.reshape(36, 512), ((0, 28), (0, 0)))
    bias = gate_bias.reshape(1, 512)
    hidden = hidden_init[0]
    rain = rain[0]
    cell = cell_init.reshape(512, 128)
    row = ((128, 128), F32)

    to_a, to_b = call(border_kernel, 2, [((136, 128), BF16)] * 2)(side, hidden, rain)
    new, to_a, to_b, cell_new, gates, mask, taps0, taps1, wide0 = call(
        first_kernel,
        9,
        [
            ((4, 128, 128), BF16), ((128, 128), BF16), ((128, 128), BF16), ((512, 128), F32),
            ((512, 512), F32), ((512, 128), F32), ((64, 512), BF16), ((64, 512), BF16),
            ((768, 384), BF16),
        ],
        [((6, 128, 128), BF16), ((24, 128), F32), ((64, 512), F32), ((512, 512), F32)],
    )(side, hidden, swap(to_a), across(to_b), rain, weight, rain_lines, bias, cell, land_mask)
    final, grad1, grad_cell, to_a, to_b, wide1 = call(
        second_kernel,
        10,
        [
            ((4, 128, 128), BF16), ((512, 512), BF16), ((512, 128), F32), row, row,
            ((768, 384), BF16),
        ],
        [((6, 128, 128), BF16), ((512, 512), F32), ((2, 128, 128), F32)],
    )(
        side, new, swap(to_a), across(to_b), taps1, weight, rain_lines, bias, cell_new, mask,
        cotangent[0, 1],
    )
    from_a, from_b = (swap(to_a), across(to_b))
    pile = ((2, LINES, 128), F32)
    kept, given, own = call(
        third_kernel, 4, [pile, pile, ((4, 128, 128), F32)], [((512, 384), F32)]
    )(side, grad1, weight, wide1, taps1)
    kept, given, grad0, to_a, to_b = call(
        fourth_kernel,
        14,
        [pile, pile, ((512, 512), BF16), row, row],
        [((4, 128, 128), F32), ((2, 128, 128), F32)],
        {1: 0, 2: 1},
    )(
        side, kept, given, own, from_a, from_b, cotangent[0, 0], gates, cell, cell_new, mask,
        grad_cell, weight, wide0, taps0,
    )
    got, from_a, from_b = lax.optimization_barrier((swap(given), swap(to_a), across(to_b)))
    last = lambda grad: call(last_kernel, 4, [((4, 128, 128), F32)], [((512, 384), F32)])(
        side, grad, weight, from_a, from_b
    )[0]
    grad_hidden, grad_w_hidden, grad_w_rain, grad_bias = sum_everywhere(
        side, kept, got, swap, (grad0, last)
    )
    return (
        final[None],
        grad_hidden[None],
        grad_w_hidden.reshape(hidden_weight.shape),
        grad_w_rain,
        grad_bias.reshape(gate_bias.shape),
    )


def solution(mesh):
    in_specs = (
        P("event", None, "space", None, None),
        P("event", "space", None, None),
        P("event", "space", None, None),
        P("space", None),
        P(),
        P(),
        P(),
        P("event", None, "space", None, None),
    )
    out_specs = (P("event", "space", None, None), P("event", "space", None, None), P(), P(), P())
    return jax.shard_map(
        on_device, mesh=mesh, in_specs=in_specs, out_specs=out_specs, check_vma=False
    )
```
